256 devices in a mesh: dp: 8 (over x, y_lo), tensor: 32 (over z, y_hi, core).
Axes of the slice: x: 4, y: 4 (y_hi: 2, y_lo: 2; y = y_hi * 2 + y_lo), z: 8, core: 2. Of those that a mesh axis runs over, the one named last changes fastest.
Arguments:
- real_feats: bfloat16 [16384, 1536], P(('dp', 'tensor')), may hold values from -6 to 6
- fake_feats: bfloat16 [16384, 1536], P(('dp', 'tensor')), may hold values from -6 to 6
- mix_num: int32 [16384], P(('dp', 'tensor')), may hold values from 0 to 256
- w_first: bfloat16 [1536, 12288], P(None, 'tensor'), may hold values from -0.15625 to 0.15625
- bias: float32 [12288], P('tensor'), may hold values from -3 to 3
- head: float32 [12288], P('tensor'), may hold values from -0.0546875 to 0.0546875
Outputs:
- grad_w: float32 [1536, 12288], P('dp', 'tensor')
- grad_bias: float32 [12288], P('tensor')
- grad_head: float32 [12288], P('tensor')
- penalty: float32 [], replicated
The draws below stay inside these ranges and needn't reach their ends.
All inputs are finite; a program needn't handle non-finite values.
Results may differ from the reference program's by a relative error of at most 0.0005.
Values may be sent and summed in bfloat16 or wider, within the bound.
No kernel may reach another device: no remote copies, remote signals or barrier semaphores. Data moves between devices by JAX's collectives and lax.ppermute only.
A program may use at most 64 MiB of HBM per device.

```python
import jax
import jax.numpy as jnp
from jax import lax

D = 1536
H = 12288
ROWS = 16384
BLOCK = 2048


def plant(entries, rng, smallest, high):
    longest = entries.shape.index(max(entries.shape))
    spots = []
    for shift in (0, 1):
        where = [jax.random.randint(jax.random.fold_in(rng, axis), (), 0, length) for axis, length in enumerate(entries.shape)]
        where[longest] = (where[longest] + shift) % entries.shape[longest]
        spots.append(tuple(where))
    return entries.at[spots[0]].set(smallest).at[spots[1]].set(high)


def steps_of(own_key, extent, split, smallest, high):
    level, own = 1.0, jax.random.fold_in(own_key, 6)
    for axis_at, blocks in split:
        steps = jnp.exp(jax.random.uniform(jax.random.fold_in(own, axis_at), (blocks,), jnp.float32, smallest / len(split), high / len(split)))
        level = level * jnp.repeat(steps, extent[axis_at] // blocks).reshape([-1 if axis == axis_at else 1 for axis in range(len(extent))])
    return level


def centred(key, shape, deviation, bound, cuts=(), held_as=jnp.bfloat16):
    gain = steps_of(key, shape, cuts, -0.22, 0.18) if cuts else 1.0
    drawn = jax.random.normal(key, shape, jnp.float32) * deviation * gain
    return jnp.minimum(jnp.maximum(drawn, -bound), bound).astype(held_as)


def setup_inputs(seed: int = 0) -> dict:
    keys = jax.random.split(jax.random.key(seed), 7)
    real_feats = centred(keys[0], (ROWS, D), 1.0, 6.0, ((0, 256),))
    fake_feats = centred(keys[1], (ROWS, D), 1.0, 6.0, ((0, 256),))
    mix_num = plant(jax.random.randint(keys[2], (ROWS,), 0, 257), jax.random.fold_in(keys[2], 1), 0, 256).astype(jnp.int32)
    w_first = centred(keys[3], (D, H), D ** -0.5, 0.15625, ((1, 32),))
    bias = centred(keys[4], (H,), 0.5, 3.0, ((0, 32),), jnp.float32)
    head = centred(keys[5], (H,), H ** -0.5, 0.0546875, ((0, 32),), jnp.float32)
    return dict(real_feats=real_feats, fake_feats=fake_feats, mix_num=mix_num, w_first=w_first, bias=bias, head=head)


def block_terms(real_rows, fake_rows, mix_rows, w_first, bias, head):
    coef = mix_rows.astype(jnp.float32) / 256.0
    real_f = real_rows.astype(jnp.float32)
    mixed = (real_f + coef[:, None] * (fake_rows.astype(jnp.float32) - real_f)).astype(jnp.bfloat16)
    z = jnp.dot(mixed, w_first, preferred_element_type=jnp.float32) + bias
    sg = jax.nn.sigmoid(z)
    d1 = sg * (1.0 + z * (1.0 - sg))
    d2 = sg * (1.0 - sg) * (2.0 + z * (1.0 - 2.0 * sg))
    u = (d1 * head).astype(jnp.bfloat16)
    g = jnp.dot(u, w_first.T, preferred_element_type=jnp.float32)
    norm = jnp.sqrt(lax.optimization_barrier(jnp.sum(g * g, axis=1)) + 1e-06)
    scale = 20.0 * (norm - 1.0) / norm
    big = (scale[:, None] * g).astype(jnp.bfloat16)
    loss = jnp.sum((norm - 1.0) ** 2)
    p = jnp.dot(big, w_first, preferred_element_type=jnp.float32)
    dz = p * head * d2
    dzb = dz.astype(jnp.bfloat16)
    grad_w = jnp.dot(mixed.T, dzb, preferred_element_type=jnp.float32) + jnp.dot(big.T, u, preferred_element_type=jnp.float32)
    return (grad_w, lax.optimization_barrier(jnp.sum(dz, axis=0)), lax.optimization_barrier(jnp.sum(p * d1, axis=0)), loss)

def reference(real_feats, fake_feats, mix_num, w_first, bias, head):
    count = ROWS // BLOCK
    real_b = real_feats.reshape(count, BLOCK, D)
    fake_b = fake_feats.reshape(count, BLOCK, D)
    mix_b = mix_num.reshape(count, BLOCK)

    def step(carry, items):
        gw, gb, gh, total = block_terms(items[0], items[1], items[2], w_first, bias, head)
        return ((carry[0] + gw, carry[1] + gb, carry[2] + gh, carry[3] + total), None)
    init = (jnp.zeros((D, H), jnp.float32), jnp.zeros((H,), jnp.float32), jnp.zeros((H,), jnp.float32), jnp.zeros((), jnp.float32))
    sums, _ = lax.scan(step, init, (real_b, fake_b, mix_b))
    penalty = 10.0 * sums[3] / ROWS
    return (sums[0], sums[1], sums[2], penalty)
```

```python
import jax
import jax.numpy as jnp
from jax import lax
from jax.sharding import Mesh
from jax.sharding import PartitionSpec as P

ALL = ("x", "yl", "z", "yh", "c")
Y = ("yl", "yh")
F32 = jnp.float32
BF16 = jnp.bfloat16


def ring(n, step):
    return [(i, (i + step) % n) for i in range(n)]


def y_swap(dl, dh):
    return [(l * 2 + h, (l ^ dl) * 2 + (h ^ dh)) for l in range(2) for h in range(2)]


CORE = [(0, 1), (1, 0)]


def z_next(a):
    return lax.ppermute(a, "z", ring(8, -1))


def z_prev(a):
    return lax.ppermute(a, "z", ring(8, 1))


def core(a):
    return lax.ppermute(a, "c", CORE)


def across(a):
    return lax.ppermute(a, Y, y_swap(1, 1))


def within(a):
    return lax.ppermute(a, Y, y_swap(1, 0))


def gather_z(block):
    half = block.shape[0] // 2
    nxt, prv = [block], [block]
    for _ in range(3):
        nxt.append(z_next(nxt[-1]))
        prv.append(z_prev(prv[-1]))
    far = [z_next(nxt[3][:half]), z_prev(prv[3][half:])]
    return jnp.concatenate([block, nxt[1], prv[1], nxt[2], prv[2], nxt[3], prv[3], *far], axis=0)


def scatter_z(parts):
    rows = parts.shape[0] // 8
    half = rows // 2
    own, n1, p1, n2, p2, n3, p3, far = (parts[i * rows : (i + 1) * rows] for i in range(8))
    up = z_prev(far[:half].astype(BF16)).astype(F32)
    down = z_next(far[half:].astype(BF16)).astype(F32)
    up = jnp.concatenate([n3[:half] + up, n3[half:]], axis=0)
    down = jnp.concatenate([p3[:half], p3[half:] + down], axis=0)
    for n, p in ((n2, p2), (n1, p1), (own, None)):
        up = z_prev(up.astype(BF16)).astype(F32)
        down = z_next(down.astype(BF16)).astype(F32)
        if p is None:
            return n + (up + down)
        up = n + up
        down = p + down


def ring4(own, plus, minus, far, to_plus, to_minus, turn):
    half = far.shape[0] // 2
    a = to_plus(far[:half])
    b = to_minus(far[half:])
    if turn:
        plus, minus = minus, plus
    plus = jnp.concatenate([plus[:half] + a, plus[half:]], axis=0)
    minus = jnp.concatenate([minus[:half], minus[half:] + b], axis=0)
    if turn:
        plus, minus = minus, plus
    return own + to_plus(plus) + to_minus(minus)


def total_xy(v):
    v = v + within(v)
    v = v + lax.ppermute(v, "x", [(i, i ^ 1) for i in range(4)])
    return v + lax.ppermute(v, "x", [(i, i ^ 2) for i in range(4)])


def contract(a, b, dims):
    return lax.dot_general(a, b, (dims, ((), ())), preferred_element_type=F32)


def scatter_w(part):
    d, cols = part.shape[0], part.shape[-1]
    x = lax.axis_index("x")
    yl = lax.axis_index("yl")
    blocks = part.reshape(4, 2, d // 8, 2, cols)

    def rows_of(dx):
        return lax.dynamic_index_in_dim(blocks, (x + dx) % 4, 0, keepdims=False)

    def to_x(k):
        return lambda a: lax.ppermute(a, "x", ring(4, k))

    cut = d // 16
    by_x = [rows_of(k) for k in (0, 1, 3, 2)]
    first = [b[:, :cut] for b in by_x]
    second = [b[:, cut:] for b in by_x]

    def y_cut(b, axis):
        mine = lax.dynamic_index_in_dim(b, yl, axis, keepdims=False)
        other = lax.dynamic_index_in_dim(b, 1 - yl, axis, keepdims=False)
        return mine, other

    def x_stage(own, plus, minus, far):
        return ring4(own, plus, minus, far, to_x(1), to_x(-1), False)

    def y_stage(mine, other, dim):
        def side(a, k):
            return lax.index_in_dim(a, k, dim, keepdims=False)

        return ring4(side(mine, 0), side(other, 1), side(other, 0), side(mine, 1), across, within, True)

    a = x_stage(*first)
    a = y_stage(*y_cut(a, 0), 1)
    both = jnp.stack(second, 0)
    mine, other = y_cut(both, 1)
    mine, other = jnp.moveaxis(mine, 0, 1), jnp.moveaxis(other, 0, 1)
    b = y_stage(mine, other, 2)
    b = x_stage(*(b[:, k] for k in range(4)))
    return jnp.concatenate([a, b], axis=0)


def local(real_feats, fake_feats, mix_num, w_first, bias, head):
    coef = mix_num.astype(F32) / 256.0
    real_f = real_feats.astype(F32)
    mixed = (real_f + coef[:, None] * (fake_feats.astype(F32) - real_f)).astype(BF16)
    w_far = across(w_first)
    w = jnp.concatenate([w_first, core(w_first), w_far, core(w_far)], axis=1)
    vec = jnp.stack([bias, head])
    vec = jnp.concatenate([vec, core(vec)], axis=1)
    vec = jnp.concatenate([vec, across(vec)], axis=1)
    bias, head = vec[0], vec[1]
    group = gather_z(mixed)
    z = contract(group, w, ((1,), (0,))) + bias
    sg = jax.nn.sigmoid(z)
    d1 = sg * (1.0 + z * (1.0 - sg))
    d2 = sg * (1.0 - sg) * (2.0 + z * (1.0 - 2.0 * sg))
    u = (d1 * head).astype(BF16)
    g = scatter_z(contract(u, w, ((1,), (1,))))
    norm = jnp.sqrt(jnp.sum(g * g, axis=1) + 1e-06)
    scale = 20.0 * (norm - 1.0) / norm
    loss = jnp.sum((norm - 1.0) ** 2)
    big = gather_z((scale[:, None] * g).astype(BF16))
    p = contract(big, w, ((1,), (0,)))
    dz = p * head * d2
    dzb = dz.astype(BF16)
    cols = w_first.shape[1]
    sums = jnp.stack([jnp.sum(dz, axis=0), jnp.sum(p * d1, axis=0)])
    sums = sums.reshape(2, 2, 2, cols)
    sums = sums[:, :, 0] + core(sums[:, :, 1])
    sums = sums[:, 0] + across(sums[:, 1])
    sums = total_xy(sums)
    loss = jnp.full((8, 128), loss, F32)
    loss = loss + core(loss)
    loss = loss + across(loss)
    loss = total_xy(loss)
    for k in (1, 2, 4):
        loss = loss + lax.ppermute(loss, "z", [(i, i ^ k) for i in range(8)])
    total_rows = mixed.shape[0] * 256
    penalty = 10.0 * loss[0, 0] / total_rows
    part = contract(group, dzb, ((0,), (0,))) + contract(big, u, ((0,), (0,)))
    part = part.reshape(part.shape[0], 2, 2, cols)
    part = part[:, :, 0] + core(part[:, :, 1])
    return (scatter_w(part), sums[0], sums[1], penalty)


def solution(mesh):
    torus = Mesh(mesh.devices.reshape(4, 2, 8, 2, 2), ALL)
    return jax.shard_map(
        local,
        mesh=torus,
        in_specs=(
            P(ALL, None),
            P(ALL, None),
            P(ALL),
            P(None, ("z", "yh", "c")),
            P(("z", "yh", "c")),
            P(("z", "yh", "c")),
        ),
        out_specs=(
            P(("x", "yl"), ("z", "yh", "c")),
            P(("z", "yh", "c")),
            P(("z", "yh", "c")),
            P(),
        ),
        check_vma=False,
    )
```

```python
import jax
import jax.numpy as jnp
from jax import lax
from jax.sharding import Mesh
from jax.sharding import PartitionSpec as P

ALL = ("x", "yl", "z", "yh", "c")
Y = ("yl", "yh")
F32 = jnp.float32
BF16 = jnp.bfloat16


def y_swap(dl, dh):
    return [(i * 2 + j, (i ^ dl) * 2 + (j ^ dh)) for i in range(2) for j in range(2)]


def z_turn(step):
    return [(z * 2 + c, (z + (step if c == 0 else -step)) % 8 * 2 + c) for z in range(8) for c in range(2)]


def out_z(a):
    return lax.ppermute(a, ("z", "c"), z_turn(1))


def back_z(a):
    return lax.ppermute(a, ("z", "c"), z_turn(-1))


def core(a):
    return lax.ppermute(a, "c", [(0, 1), (1, 0)])


def across(a):
    return lax.ppermute(a, Y, y_swap(1, 1))


def within(a):
    return lax.ppermute(a, Y, y_swap(1, 0))


def x_up(a):
    return lax.ppermute(a, "x", [(i, (i + 1) % 4) for i in range(4)])


def x_down(a):
    return lax.ppermute(a, "x", [(i, (i - 1) % 4) for i in range(4)])


def gather_z(block):
    own, other = [block], [core(block)]
    for _ in range(3):
        own.append(out_z(own[-1]))
        other.append(out_z(other[-1]))
    own.append(out_z(own[-1]))
    mine = [own[1], other[1], own[2], other[2], own[3], other[3], own[4]]
    return [own[0], other[0], *mine, *(core(a) for a in mine)]


def contract(a, b, dims):
    return lax.dot_general(a, b, (dims, ((), ())), preferred_element_type=F32)


def scatter_z(u, w):
    rows = u.shape[0] // 16
    dims = ((1,), (1,))
    theirs = contract(u[9 * rows :], w, dims).astype(BF16)
    mine = contract(u[2 * rows : 9 * rows], w, dims)
    here = contract(u[: 2 * rows], w, dims)
    mine = mine + core(theirs).astype(F32)
    part = [mine[i * rows : (i + 1) * rows] for i in range(7)]
    own = part[6]
    own = part[4] + back_z(own.astype(BF16)).astype(F32)
    other = part[5]
    for k in (1, 0):
        own = part[2 * k] + back_z(own.astype(BF16)).astype(F32)
        other = part[2 * k + 1] + back_z(other.astype(BF16)).astype(F32)
    own = here[:rows] + back_z(own.astype(BF16)).astype(F32)
    other = here[rows:] + back_z(other.astype(BF16)).astype(F32)
    return own + core(other)


def ring4(own, plus, minus, far, to_plus, to_minus, turn):
    half = far.shape[0] // 2
    a = to_plus(far[:half])
    b = to_minus(far[half:])
    if turn:
        plus, minus = minus, plus
    plus = jnp.concatenate([plus[:half] + a, plus[half:]], axis=0)
    minus = jnp.concatenate([minus[:half], minus[half:] + b], axis=0)
    if turn:
        plus, minus = minus, plus
    return own + to_plus(plus) + to_minus(minus)


def split_y(piece, yl):
    mine = lax.dynamic_index_in_dim(piece, yl, 0, keepdims=False)
    other = lax.dynamic_index_in_dim(piece, 1 - yl, 0, keepdims=False)
    return mine, other


def scatter_w(lhs, rhs):
    d, cols = lhs[0].shape[1], rhs[0].shape[1] // 2
    x = lax.axis_index("x")
    yl = lax.axis_index("yl")
    width = d // 4
    half = width // 4

    def piece(dx):
        at = (x + dx) % 4 * width
        total = sum(
            contract(lax.dynamic_slice_in_dim(a, at, width, 1), b, ((0,), (0,))) for a, b in zip(lhs, rhs)
        )
        return total.reshape(2, width // 2, 2 * cols)

    far, plus, minus, own = (piece(k) for k in (2, 1, 3, 0))

    def y_stage(mine, other):
        return ring4(mine[..., :cols], other[..., cols:], other[..., :cols], mine[..., cols:], across, within, True)

    a = ring4(*(p[:, :half] for p in (own, plus, minus, far)), x_up, x_down, False)
    a = y_stage(*split_y(a, yl))
    mine, other = split_y(jnp.stack([p[:, half:] for p in (own, plus, minus, far)], 1), yl)
    b = y_stage(mine, other)
    b = ring4(*(b[k] for k in range(4)), x_up, x_down, False)
    return jnp.concatenate([a, b], axis=0)


def local(real_feats, fake_feats, mix_num, w_first, bias, head):
    cols = w_first.shape[1]
    coef = mix_num.astype(F32) / 256.0
    real_f = real_feats.astype(F32)
    mixed = (real_f + coef[:, None] * (fake_feats.astype(F32) - real_f)).astype(BF16)
    vec = jnp.stack([bias, head])
    vec = jnp.concatenate([vec, across(vec)], axis=1)
    bias, head = vec[0], vec[1]
    group = jnp.concatenate(gather_z(mixed), axis=0)
    w = jnp.concatenate([w_first, across(w_first)], axis=1)
    z = contract(group, w, ((1,), (0,))) + bias
    sg = jax.nn.sigmoid(z)
    d1 = sg * (1.0 + z * (1.0 - sg))
    d2 = sg * (1.0 - sg) * (2.0 + z * (1.0 - 2.0 * sg))
    u = (d1 * head).astype(BF16)
    g = scatter_z(u, w)
    norm = jnp.sqrt(jnp.sum(g * g, axis=1) + 1e-06)
    scale = 20.0 * (norm - 1.0) / norm
    loss = jnp.sum((norm - 1.0) ** 2)
    big = jnp.concatenate(gather_z((scale[:, None] * g).astype(BF16)), axis=0)
    loss = sum(gather_z(jnp.full((1, cols), loss, F32)))
    p = contract(big, w, ((1,), (0,)))
    dz = p * head * d2
    dzb = dz.astype(BF16)
    sums = jnp.stack([jnp.sum(dz, axis=0), jnp.sum(p * d1, axis=0)])
    sums = jnp.concatenate([sums, jnp.concatenate([loss, loss], axis=1)], axis=0)
    sums = sums[:, :cols] + across(sums[:, cols:])
    sums = sums + within(sums)
    above, below = x_up(sums), x_down(sums)
    sums = sums + above + below + x_up(above)
    total_rows = mixed.shape[0] * 256
    penalty = 10.0 * sums[2, 0] / total_rows
    grad_w = scatter_w((group, big), (dzb, u))
    return (grad_w, sums[0], sums[1], penalty)


def solution(mesh):
    torus = Mesh(mesh.devices.reshape(4, 2, 8, 2, 2), ALL)
    hidden = ("z", "yh", "c")
    return jax.shard_map(
        local,
        mesh=torus,
        in_specs=(P(ALL, None), P(ALL, None), P(ALL), P(None, hidden), P(hidden), P(hidden)),
        out_specs=(P(("x", "yl"), hidden), P(hidden), P(hidden), P()),
        check_vma=False,
    )
```

```python
import jax
import jax.numpy as jnp
from jax import lax
from jax.sharding import Mesh
from jax.sharding import PartitionSpec as P

ALL = ("x", "yl", "z", "yh", "c")
Y = ("yl", "yh")
F32 = jnp.float32
BF16 = jnp.bfloat16


def y_swap(dl, dh):
    return [(i * 2 + j, (i ^ dl) * 2 + (j ^ dh)) for i in range(2) for j in range(2)]


def z_turn(step):
    return [(z * 2 + c, (z + (step if c == 0 else -step)) % 8 * 2 + c) for z in range(8) for c in range(2)]


def out_z(a):
    return lax.ppermute(a, ("z", "c"), z_turn(1))


def back_z(a):
    return lax.ppermute(a, ("z", "c"), z_turn(-1))


def core(a):
    return lax.ppermute(a, "c", [(0, 1), (1, 0)])


def across(a):
    return lax.ppermute(a, Y, y_swap(1, 1))


def within(a):
    return lax.ppermute(a, Y, y_swap(1, 0))


def y_far(a):
    return lax.ppermute(a, Y, y_swap(0, 1))


def x_up(a):
    return lax.ppermute(a, "x", [(i, (i + 1) % 4) for i in range(4)])


def x_down(a):
    return lax.ppermute(a, "x", [(i, (i - 1) % 4) for i in range(4)])


def x_far(a):
    return lax.ppermute(a, "x", [(i, i ^ 2) for i in range(4)])


tie = lax.optimization_barrier


def contract(a, b, dims):
    return lax.dot_general(a, b, (dims, ((), ())), preferred_element_type=F32)


def gather_z(block, extra=None):
    own, other = block, core(block)
    yield [own, other], extra
    for step in range(4):
        if step < 3:
            if extra is None:
                own, other = tie((own, other))
            else:
                own, other, extra = tie((own, other, extra))
                extra = out_z(extra)
            own, other = out_z(own), out_z(other)
            yield [own, other, core(own), core(other)], extra
        else:
            if extra is not None:
                own, extra = tie((own, extra))
                extra = out_z(extra)
            own = out_z(own)
            yield [own, core(own)], extra


def scatter_z(us, w):
    dims = ((1,), (1,))
    mine, theirs = [], []
    for u in us[:0:-1]:
        half = u.shape[0] // 2
        theirs.append(core(contract(u[half:], w, dims).astype(BF16)))
        mine.append(contract(u[:half], w, dims))
    here = contract(us[0], w, dims)
    rows = here.shape[0] // 2
    parts = [m + t.astype(F32) for m, t in zip(mine, theirs)]
    own = back_z(parts[0].astype(BF16)).astype(F32)
    own, other = parts[1][:rows] + own, parts[1][rows:]
    for part in (parts[2], parts[3], here):
        own, other = tie((own.astype(BF16), other.astype(BF16)))
        own = part[:rows] + back_z(own).astype(F32)
        other = part[rows:] + back_z(other).astype(F32)
    return own + core(other)


def share_w(w_first):
    half = w_first.shape[0] // 2
    width = half // 4
    x = lax.axis_index("x").astype(jnp.uint32)
    quarter = across(lax.dynamic_slice_in_dim(w_first, half + x * width, width, 0))
    direct = across(w_first[:half])

    def spread(quarter):
        parts = [quarter, x_down(quarter), x_up(quarter), x_far(quarter)]
        shared = jnp.zeros((4, *quarter.shape), quarter.dtype)
        for k, part in zip((0, 1, 3, 2), parts):
            shared = lax.dynamic_update_index_in_dim(shared, part, (x + k) & 3, 0)
        return jnp.concatenate([direct, shared.reshape(half, -1)], axis=0)

    return quarter, spread


def scatter_w(lhs, rhs, sums):
    d, cols = lhs[0].shape[1], rhs[0].shape[1] // 2
    x = lax.axis_index("x").astype(jnp.uint32)
    yl = lax.axis_index("yl").astype(jnp.uint32)
    width = d // 4
    half = width // 4

    def piece(dx):
        at = ((x + dx) & 3) * width
        total = sum(
            contract(lax.dynamic_slice_in_dim(a, at, width, 1), b, ((0,), (0,))) for a, b in zip(lhs, rhs)
        )
        return total.reshape(2, width // 2, 2 * cols)

    def split_y(p):
        mine = lax.dynamic_index_in_dim(p, yl, 0, keepdims=False)
        other = lax.dynamic_index_in_dim(p, 1 - yl, 0, keepdims=False)
        return mine[..., :cols], other[..., cols:], other[..., :cols], mine[..., cols:]

    def y_stage(p):
        here, over, near, far = split_y(p)
        far = y_far(far)
        return here + across(over) + within(near) + far

    far = piece(2)
    far, sums = tie((far, sums))
    plus, minus, own = (piece(k) for k in (1, 3, 0))
    a = x_far(far[:, :half])
    a = own[:, :half] + x_up(plus[:, :half]) + x_down(minus[:, :half]) + a
    b = y_stage(jnp.stack([p[:, half:] for p in (own, plus, minus, far)], 1))
    a = y_stage(a)
    b_far = x_far(b[3])
    b = b[0] + x_up(b[1]) + x_down(b[2]) + b_far
    sums = sums[:, :cols] + across(sums[:, cols:])
    sums = sums + within(sums)
    sums = sums + x_up(sums) + x_down(sums) + x_far(sums)
    return jnp.concatenate([a, b], axis=0), sums


def local(real_feats, fake_feats, mix_num, w_first, bias, head):
    cols = w_first.shape[1]
    quarter, spread = share_w(w_first)
    vec = jnp.stack([bias, head])
    vec = jnp.concatenate([vec, across(vec)], axis=1)
    bias, head = vec[0], vec[1]
    coef = mix_num.astype(F32) / 256.0
    real_f = real_feats.astype(F32)
    mixed = (real_f + coef[:, None] * (fake_feats.astype(F32) - real_f)).astype(BF16)

    group = []
    for step, (blocks, _) in enumerate(gather_z(mixed)):
        if step == 1:
            tied = tie((*blocks[:2], quarter))
            quarter = tied[2]
        group.append(jnp.concatenate(blocks, axis=0))
    w = jnp.concatenate([w_first, spread(quarter)], axis=1)
    us, d1s, d2s = [], [], []
    for chunk in group:
        z = contract(chunk, w, ((1,), (0,))) + bias
        sg = jax.nn.sigmoid(z)
        d1 = sg * (1.0 + z * (1.0 - sg))
        d1s.append(d1)
        d2s.append(sg * (1.0 - sg) * (2.0 + z * (1.0 - 2.0 * sg)))
        us.append((d1 * head).astype(BF16))
    g = scatter_z(us, w)
    norm = jnp.sqrt(jnp.sum(g * g, axis=1) + 1e-06)
    scale = 20.0 * (norm - 1.0) / norm
    loss = jnp.full((1, cols), jnp.sum((norm - 1.0) ** 2), F32)
    loss = loss + core(loss)
    bigs, dzs, sums, losses = [], [], 0.0, []
    steps = gather_z((scale[:, None] * g).astype(BF16), loss)
    for (blocks, loss), d1, d2 in zip(steps, d1s, d2s):
        losses.append(loss)
        bigs.append(jnp.concatenate(blocks, axis=0))
        p = contract(bigs[-1], w, ((1,), (0,)))
        dz = p * head * d2
        dzs.append(dz.astype(BF16))
        sums = sums + jnp.stack([jnp.sum(dz, axis=0), jnp.sum(p * d1, axis=0)])
    mine = losses[1] + losses[2] + losses[3] + 0.5 * losses[4]
    loss = losses[0] + mine + core(mine)
    sums = jnp.concatenate([sums, jnp.concatenate([loss, loss], axis=1)], axis=0)
    lhs = [jnp.concatenate(a, axis=0) for a in (group, bigs)]
    rhs = [jnp.concatenate(a, axis=0) for a in (dzs, us)]
    grad_w, sums = scatter_w(lhs, rhs, sums)
    penalty = 10.0 * sums[2, 0] / (mixed.shape[0] * 256)
    return (grad_w, sums[0], sums[1], penalty)


def solution(mesh):
    torus = Mesh(mesh.devices.reshape(4, 2, 8, 2, 2), ALL)
    hidden = ("z", "yh", "c")
    return jax.shard_map(
        local,
        mesh=torus,
        in_specs=(P(ALL, None), P(ALL, None), P(ALL), P(None, hidden), P(hidden), P(hidden)),
        out_specs=(P(("x", "yl"), hidden), P(hidden), P(hidden), P()),
        check_vma=False,
    )
```

```python
import jax
import jax.numpy as jnp
from jax import lax
from jax.sharding import Mesh
from jax.sharding import PartitionSpec as P

ALL = ("x", "yl", "z", "yh", "c")
Y = ("yl", "yh")
F32 = jnp.float32
BF16 = jnp.bfloat16


def y_swap(dl, dh):
    return [(i * 2 + j, (i ^ dl) * 2 + (j ^ dh)) for i in range(2) for j in range(2)]


def z_turn(step):
    return [(z * 2 + c, (z + (step if c == 0 else -step)) % 8 * 2 + c) for z in range(8) for c in range(2)]


def out_z(a):
    return lax.ppermute(a, ("z", "c"), z_turn(1))


def back_z(a):
    return lax.ppermute(a, ("z", "c"), z_turn(-1))


def core(a):
    return lax.ppermute(a, "c", [(0, 1), (1, 0)])


def across(a):
    return lax.ppermute(a, Y, y_swap(1, 1))


def within(a):
    return lax.ppermute(a, Y, y_swap(1, 0))


def y_far(a):
    return lax.ppermute(a, Y, y_swap(0, 1))


def x_up(a):
    return lax.ppermute(a, "x", [(i, (i + 1) % 4) for i in range(4)])


def x_down(a):
    return lax.ppermute(a, "x", [(i, (i - 1) % 4) for i in range(4)])


def x_far(a):
    return lax.ppermute(a, "x", [(i, i ^ 2) for i in range(4)])


tie = lax.optimization_barrier


def join(*arrays):
    return jnp.concatenate(arrays, axis=0)


def contract(a, b, dims):
    return lax.dot_general(a, b, (dims, ((), ())), preferred_element_type=F32)


def gather_z(chip, rows, early=None):
    hops = [chip]
    for step in range(3):
        hops.append(out_z(hops[-1]))
        if step == 0 and early is not None:
            hops[1], early = tie((hops[1], early))
    far = hops[3][:rows]
    if chip.shape[0] > 2 * rows:
        far = join(far, hops[3][2 * rows :])
    hops.append(out_z(far))
    near = join(hops[1][: 2 * rows], hops[2][: 2 * rows])
    last = join(hops[3][: 2 * rows], hops[4][:rows])
    return join(chip[: 2 * rows], near, last, core(near), core(last)), hops, early


def scatter_z(u, w, rows):
    dims = ((1,), (1,))

    def send(a):
        return back_z(a.astype(BF16)).astype(F32)

    theirs = core(contract(u[9 * rows :], w, dims).astype(BF16)).astype(F32)
    part = contract(u[2 * rows : 9 * rows], w, dims) + theirs
    passed = send(part[6 * rows :])
    passed = send(join(part[4 * rows : 5 * rows] + passed, part[5 * rows : 6 * rows]))
    passed = send(part[2 * rows : 4 * rows] + passed)
    passed = send(part[: 2 * rows] + passed)
    part = contract(u[: 2 * rows], w, dims) + passed
    return part[:rows] + core(part[rows:])


def scatter_w(lhs, rhs, sums, place):
    d, cols = lhs[0].shape[1], rhs[0].shape[1] // 2
    width = d // 4
    half = width // 4

    def piece(dx):
        total = sum(
            contract(lax.dynamic_slice_in_dim(a, place[dx], width, 1), b, ((0,), (0,))) for a, b in zip(lhs, rhs)
        )
        return total.reshape(2, width // 2, 2 * cols)

    def split_y(p):
        mine = lax.dynamic_index_in_dim(p, place[4], 0, keepdims=False)
        other = lax.dynamic_index_in_dim(p, place[5], 0, keepdims=False)
        return mine[..., :cols], other[..., cols:], other[..., :cols], mine[..., cols:]

    def first(p):
        return join(p[:, :half].reshape(2 * half, 2 * cols), sums)

    far, plus, minus, own = (piece(k) for k in (2, 1, 3, 0))
    a = (x_far(first(far)), x_up(first(plus)), x_down(first(minus)))
    b_here, b_over, b_near, b_far = split_y(jnp.stack([p[:, half:] for p in (own, plus, minus, far)], 1))
    b = (y_far(b_far), across(b_over), within(b_near))
    a, b = tie((a, b))
    a = first(own) + a[0] + a[1] + a[2]
    b = b_here + b[0] + b[1] + b[2]
    sums = a[2 * half :]
    here, over, near, far = split_y(a[: 2 * half].reshape(2, half, 2 * cols))
    low, high = sums[:, :cols], sums[:, cols:]
    a = (y_far(join(far, high)), across(join(over, high)), within(join(near, low)))
    b_rest = (x_far(b[3]), x_up(b[1]), x_down(b[2]))
    a, b_rest = tie((a, b_rest))
    a = join(here, low) + a[0] + a[1] + a[2]
    b = b[0] + b_rest[0] + b_rest[1] + b_rest[2]
    return join(a[:half], b), a[half:]


def as_terms(value, width):
    high = lax.reduce_precision(value, 8, 7)
    mid = lax.reduce_precision(value - high, 8, 7)
    low = value - high - mid
    lane = lax.broadcasted_iota(jnp.int32, value.shape, 1)
    terms = jnp.where(lane == 0, high, jnp.where(lane == 1, mid, jnp.where(lane == 2, low, 0.0)))
    return jnp.pad(terms, ((0, 15), (0, width - value.shape[1]))).astype(BF16)


def local(real_feats, fake_feats, mix_num, w_first, bias, head):
    rows, d = real_feats.shape
    cols = w_first.shape[1]
    w = jnp.concatenate([w_first, across(w_first)], axis=1)
    coef = mix_num.astype(F32) / 256.0
    real_f = real_feats.astype(F32)
    mixed = (real_f + coef[:, None] * (fake_feats.astype(F32) - real_f)).astype(BF16)
    vec = jnp.concatenate([bias, head])[None]
    far = across(vec)
    bias = jnp.concatenate([bias, far[0, :cols]])
    head = jnp.concatenate([head, far[0, cols:]])
    place = [lax.axis_index(k).astype(jnp.uint32) for k in ("x", "yl")]
    place = [((place[0] + k) & 3) * (d // 4) for k in range(4)] + [place[1], 1 - place[1]]
    group, _, place = gather_z(join(mixed, core(mixed)), rows, place)
    z = contract(group, w, ((1,), (0,))) + bias
    sg = jax.nn.sigmoid(z)
    d1 = sg * (1.0 + z * (1.0 - sg))
    d2 = sg * (1.0 - sg) * (2.0 + z * (1.0 - 2.0 * sg))
    u = (d1 * head).astype(BF16)
    g = scatter_z(u, w, rows)
    norm = jnp.sqrt(jnp.sum(g * g, axis=1, keepdims=True) + 1e-06)
    scale = 20.0 * (norm - 1.0) / norm
    loss = jnp.sum(jnp.broadcast_to((norm - 1.0) ** 2, (rows, 128)), axis=0, keepdims=True)
    mine = join((scale * g).astype(BF16), as_terms(loss, d))
    other = core(mine)
    tail = mine[rows:] + jnp.pad(other[rows:, :-3], ((0, 0), (3, 0)))
    big, hops, _ = gather_z(join(mine[:rows], other[:rows], tail), rows)
    p = contract(big, w, ((1,), (0,)))
    dz = p * head * d2
    passed = sum(a[2 * rows : 2 * rows + 1, :128].astype(F32) for a in hops[1:4])
    ends = hops[0][2 * rows : 2 * rows + 1, :128].astype(F32) + hops[4][rows : rows + 1, :128].astype(F32)
    loss = jnp.pad(ends + passed + core(passed), ((0, 5), (0, cols - 128)))
    loss = jnp.concatenate([loss, loss], axis=1)
    sums = join(jnp.sum(dz, axis=0, keepdims=True), jnp.sum(p * d1, axis=0, keepdims=True), loss)
    grad_w, sums = scatter_w((group, big), (dz.astype(BF16), u), sums, place)
    penalty = 10.0 * jnp.sum(sums[2]) / (rows * 256)
    return (grad_w, sums[0], sums[1], penalty)


def solution(mesh):
    torus = Mesh(mesh.devices.reshape(4, 2, 8, 2, 2), ALL)
    hidden = ("z", "yh", "c")
    return jax.shard_map(
        local,
        mesh=torus,
        in_specs=(P(ALL, None), P(ALL, None), P(ALL), P(None, hidden), P(hidden), P(hidden)),
        out_specs=(P(("x", "yl"), hidden), P(hidden), P(hidden), P()),
        check_vma=False,
    )
```

```python
import jax
import jax.numpy as jnp
from jax import lax
from jax.sharding import Mesh
from jax.sharding import PartitionSpec as P


ALL = ("x", "yl", "z", "yh", "c")
Y = ("yl", "yh")
F32 = jnp.float32
BF16 = jnp.bfloat16


def y_swap(dl, dh):
    return [(i * 2 + j, (i ^ dl) * 2 + (j ^ dh)) for i in range(2) for j in range(2)]


def z_turn(step):
    return [(z * 2 + c, (z + (step if c == 0 else -step)) % 8 * 2 + c) for z in range(8) for c in range(2)]


def out_z(a):
    return lax.ppermute(a, ("z", "c"), z_turn(1))


def back_z(a):
    return lax.ppermute(a, ("z", "c"), z_turn(-1))


def core(a):
    return lax.ppermute(a, "c", [(0, 1), (1, 0)])


def across(a):
    return lax.ppermute(a, Y, y_swap(1, 1))


def within(a):
    return lax.ppermute(a, Y, y_swap(1, 0))


def y_far(a):
    return lax.ppermute(a, Y, y_swap(0, 1))


def x_up(a):
    return lax.ppermute(a, "x", [(i, (i + 1) % 4) for i in range(4)])


def x_down(a):
    return lax.ppermute(a, "x", [(i, (i - 1) % 4) for i in range(4)])


def x_far(a):
    return lax.ppermute(a, "x", [(i, i ^ 2) for i in range(4)])


tie = lax.optimization_barrier


def join(*arrays):
    return jnp.concatenate(arrays, axis=0)


def contract(a, b, dims):
    return lax.dot_general(a, b, (dims, ((), ())), preferred_element_type=F32)


def gather_z(chip, rows, early=None):
    hops = [chip]
    for step in range(3):
        hops.append(out_z(hops[-1]))
        if step == 0 and early is not None:
            hops[1], early = tie((hops[1], early))
    far = hops[3][:rows]
    if chip.shape[0] > 2 * rows:
        far = join(far, hops[3][2 * rows :])
    hops.append(out_z(far))
    near = join(hops[1][: 2 * rows], hops[2][: 2 * rows])
    last = join(hops[3][: 2 * rows], hops[4][:rows])
    return join(chip[: 2 * rows], near, last, core(near), core(last)), hops, early


def scatter_z(u, w, rows):
    dims = ((1,), (1,))

    def send(a):
        return back_z(a.astype(BF16)).astype(F32)

    theirs = core(contract(u[9 * rows :], w, dims).astype(BF16)).astype(F32)
    part = contract(u[2 * rows : 9 * rows], w, dims) + theirs
    passed = send(part[6 * rows :])
    passed = send(join(part[4 * rows : 5 * rows] + passed, part[5 * rows : 6 * rows]))
    passed = send(part[2 * rows : 4 * rows] + passed)
    passed = send(part[: 2 * rows] + passed)
    part = contract(u[: 2 * rows], w, dims) + passed
    return part[:rows] + core(part[rows:])


def scatter_w(lhs, rhs, sums, place):
    d, cols = lhs[0].shape[1], rhs[0].shape[1] // 2
    width = d // 4
    lead = width * 5 // 16
    rest_rows = width // 2 - lead

    def piece(dx, rhs):
        total = sum(
            contract(lax.dynamic_slice_in_dim(a, place[dx], width, 1), b, ((0,), (0,))) for a, b in zip(lhs, rhs)
        )
        return total.reshape(2, width // 2, 2 * cols)

    def split_y(p):
        mine = lax.dynamic_index_in_dim(p, place[4], 0, keepdims=False)
        other = lax.dynamic_index_in_dim(p, place[5], 0, keepdims=False)
        return mine[..., :cols], other[..., cols:], other[..., :cols], mine[..., cols:]

    def first(p):
        return p[:, :lead].reshape(2 * lead, 2 * cols)

    far = piece(2, rhs)
    send, rhs = tie((first(far), rhs))
    a = [x_far(send)]
    plus = piece(1, rhs)
    send, rhs = tie((first(plus), rhs))
    a.append(x_up(send))
    minus = piece(3, rhs)
    send, rhs = tie((first(minus), rhs))
    a.append(x_down(send))
    own = piece(0, rhs)
    b_here, b_over, b_near, b_far = split_y(jnp.stack([p[:, lead:] for p in (own, plus, minus, far)], 1))
    low, high = sums[:, :cols], sums[:, cols:]

    def flat(q, extra):
        return join(q.reshape(4 * rest_rows, cols), extra)

    b = (y_far(flat(b_far, high)), across(flat(b_over, high)), within(flat(b_near, low)))
    a, b = tie((a, b))
    a = first(own) + a[0] + a[1] + a[2]
    b = flat(b_here, low) + b[0] + b[1] + b[2]
    sums = b[4 * rest_rows :]
    b = b[: 4 * rest_rows].reshape(4, rest_rows, cols)
    here, over, near, far = split_y(a.reshape(2, lead, 2 * cols))
    a = (y_far(far), across(over), within(near))
    rest = (x_far(join(b[3], sums)), x_up(join(b[1], sums)), x_down(join(b[2], sums)))
    a, rest = tie((a, rest))
    a = here + a[0] + a[1] + a[2]
    b = join(b[0], sums) + rest[0] + rest[1] + rest[2]
    return join(a, b[:rest_rows]), b[rest_rows:]


def as_terms(value, width):
    high = lax.reduce_precision(value, 8, 7)
    mid = lax.reduce_precision(value - high, 8, 7)
    low = value - high - mid
    lane = lax.broadcasted_iota(jnp.int32, value.shape, 1)
    terms = jnp.where(lane == 0, high, jnp.where(lane == 1, mid, jnp.where(lane == 2, low, 0.0)))
    return jnp.pad(terms, ((0, 15), (0, width - value.shape[1]))).astype(BF16)


def local(real_feats, fake_feats, mix_num, w_first, bias, head):
    rows, d = real_feats.shape
    cols = w_first.shape[1]
    w_far = across(w_first)
    w = jnp.concatenate([w_first, w_far], axis=1)
    coef = mix_num.astype(F32) / 256.0
    real_f = real_feats.astype(F32)
    mixed = (real_f + coef[:, None] * (fake_feats.astype(F32) - real_f)).astype(BF16)
    vec = jnp.concatenate([bias, head])[None]
    far = across(vec)
    bias = jnp.concatenate([bias, far[0, :cols]])
    head = jnp.concatenate([head, far[0, cols:]])
    place = [lax.axis_index(k).astype(jnp.uint32) for k in ("x", "yl")]
    place = [((place[0] + k) & 3) * (d // 4) for k in range(4)] + [place[1], 1 - place[1]]
    group, _, place = gather_z(join(mixed, core(mixed)), rows, place)
    z = tie(contract(group, w, ((1,), (0,)))) + bias
    sg = jax.nn.sigmoid(z)
    d1 = sg * (1.0 + z * (1.0 - sg))
    d2 = sg * (1.0 - sg) * (2.0 + z * (1.0 - 2.0 * sg))
    u = (d1 * head).astype(BF16)
    g = scatter_z(u, w, rows)
    norm = jnp.sqrt(jnp.sum(g * g, axis=1, keepdims=True) + 1e-06)
    scale = 20.0 * (norm - 1.0) / norm
    loss = jnp.sum(tie(jnp.broadcast_to((norm - 1.0) ** 2, (rows, 128))), axis=0, keepdims=True)
    mine = join((scale * g).astype(BF16), as_terms(loss, d))
    other = core(mine)
    tail = mine[rows:] + jnp.pad(other[rows:, :-3], ((0, 0), (3, 0)))
    big, hops, _ = gather_z(join(mine[:rows], other[:rows], tail), rows)
    p = tie(contract(big, w, ((1,), (0,))))
    dz = p * head * d2
    passed = sum(a[2 * rows : 2 * rows + 1, :128].astype(F32) for a in hops[1:4])
    ends = hops[0][2 * rows : 2 * rows + 1, :128].astype(F32) + hops[4][rows : rows + 1, :128].astype(F32)
    loss = jnp.pad(ends + passed + core(passed), ((0, 5), (0, cols - 128)))
    loss = jnp.concatenate([loss, loss], axis=1)
    sums = join(jnp.sum(dz, axis=0, keepdims=True), jnp.sum(p * d1, axis=0, keepdims=True), loss)
    grad_w, sums = scatter_w((group, big), (dz.astype(BF16), u), sums, place)
    penalty = 10.0 * jnp.sum(sums[2]) / (rows * 256)
    return (grad_w, sums[0], sums[1], penalty)


def solution(mesh):
    torus = Mesh(mesh.devices.reshape(4, 2, 8, 2, 2), ALL)
    hidden = ("z", "yh", "c")

    return jax.shard_map(
        local,
        mesh=torus,
        in_specs=(P(ALL, None), P(ALL, None), P(ALL), P(None, hidden), P(hidden), P(hidden)),
        out_specs=(P(("x", "yl"), hidden), P(hidden), P(hidden), P()),
        check_vma=False,
    )
```

```python
import jax
import jax.numpy as jnp
from jax import lax
from jax.sharding import Mesh
from jax.sharding import PartitionSpec as P


ALL = ("x", "yl", "z", "yh", "c")
Y = ("yl", "yh")
F32 = jnp.float32
BF16 = jnp.bfloat16


def y_swap(dl, dh):
    return [(i * 2 + j, (i ^ dl) * 2 + (j ^ dh)) for i in range(2) for j in range(2)]


def z_turn(step):
    return [(z * 2 + c, (z + (step if c == 0 else -step)) % 8 * 2 + c) for z in range(8) for c in range(2)]


def out_z(a):
    return lax.ppermute(a, ("z", "c"), z_turn(1))


def back_z(a):
    return lax.ppermute(a, ("z", "c"), z_turn(-1))


def core(a):
    return lax.ppermute(a, "c", [(0, 1), (1, 0)])


def across(a):
    return lax.ppermute(a, Y, y_swap(1, 1))


def within(a):
    return lax.ppermute(a, Y, y_swap(1, 0))


def y_far(a):
    return lax.ppermute(a, Y, y_swap(0, 1))


def x_up(a):
    return lax.ppermute(a, "x", [(i, (i + 1) % 4) for i in range(4)])


def x_down(a):
    return lax.ppermute(a, "x", [(i, (i - 1) % 4) for i in range(4)])


def x_far(a):
    return lax.ppermute(a, "x", [(i, i ^ 2) for i in range(4)])


tie = lax.optimization_barrier


def join(*arrays):
    return jnp.concatenate(arrays, axis=0)


def contract(a, b, dims):
    return lax.dot_general(a, b, (dims, ((), ())), preferred_element_type=F32)


def gather_z(own, other, rows, early=None):
    owns, others = [own], [other]
    for step in range(3):
        owns.append(out_z(owns[-1]))
        others.append(out_z(others[-1]))
        if step == 0 and early is not None:
            owns[1], early = tie((owns[1], early))
    far = owns[3]
    if other.shape[0] > rows:
        far = join(far, others[3][rows:])
    owns.append(out_z(far))
    near = join(owns[1], others[1][:rows], owns[2], others[2][:rows])
    last = join(owns[3], others[3][:rows], owns[4][:rows])
    tails = [a[rows:] for a in (*others, owns[4])]
    return join(own, other[:rows], near, last, core(near), core(last)), tails, early


def scatter_z(u, w, rows):
    dims = ((1,), (1,))

    def send(a):
        return back_z(a.astype(BF16)).astype(F32)

    theirs = core(contract(u[9 * rows :], w, dims).astype(BF16)).astype(F32)
    part = contract(u[2 * rows : 9 * rows], w, dims) + theirs
    passed = send(part[6 * rows :])
    passed = send(join(part[4 * rows : 5 * rows] + passed, part[5 * rows : 6 * rows]))
    passed = send(part[2 * rows : 4 * rows] + passed)
    passed = send(part[: 2 * rows] + passed)
    part = contract(u[: 2 * rows], w, dims) + passed
    return part[:rows] + core(part[rows:])


def scatter_w(lhs, rhs, sums, place):
    d, cols = lhs[0].shape[1], rhs[0].shape[1] // 2
    width = d // 4
    lead = width * 5 // 16
    rest_rows = width // 2 - lead

    def piece(dx, rhs):
        total = sum(
            contract(lax.dynamic_slice_in_dim(a, place[dx], width, 1), b, ((0,), (0,))) for a, b in zip(lhs, rhs)
        )
        return total.reshape(2, width // 2, 2 * cols)

    def split_y(p):
        mine = lax.dynamic_index_in_dim(p, place[4], 0, keepdims=False)
        other = lax.dynamic_index_in_dim(p, place[5], 0, keepdims=False)
        return mine[..., :cols], other[..., cols:], other[..., :cols], mine[..., cols:]

    def first(p):
        return p[:, :lead].reshape(2 * lead, 2 * cols)

    far = piece(2, rhs)
    send, rhs = tie((first(far), rhs))
    a = [x_far(send)]
    plus = piece(1, rhs)
    send, rhs = tie((first(plus), rhs))
    a.append(x_up(send))
    minus = piece(3, rhs)
    send, rhs = tie((first(minus), rhs))
    a.append(x_down(send))
    own = piece(0, rhs)
    b_here, b_over, b_near, b_far = split_y(jnp.stack([p[:, lead:] for p in (own, plus, minus, far)], 1))
    low, high = sums[:, :cols], sums[:, cols:]

    def flat(q, extra):
        return join(q.reshape(4 * rest_rows, cols), extra)

    b = (y_far(flat(b_far, high)), across(flat(b_over, high)), within(flat(b_near, low)))
    a, b = tie((a, b))
    a = first(own) + a[0] + a[1] + a[2]
    b = flat(b_here, low) + b[0] + b[1] + b[2]
    sums = b[4 * rest_rows :]
    b = b[: 4 * rest_rows].reshape(4, rest_rows, cols)
    here, over, near, far = split_y(a.reshape(2, lead, 2 * cols))
    a = (y_far(far), across(over), within(near))
    rest = (x_far(join(b[3], sums)), x_up(join(b[1], sums)), x_down(join(b[2], sums)))
    a, rest = tie((a, rest))
    a = here + a[0] + a[1] + a[2]
    b = join(b[0], sums) + rest[0] + rest[1] + rest[2]
    return join(a, b[:rest_rows]), b[rest_rows:]


def as_terms(value, width):
    high = lax.reduce_precision(value, 8, 7)
    mid = lax.reduce_precision(value - high, 8, 7)
    low = value - high - mid
    lane = lax.broadcasted_iota(jnp.int32, value.shape, 1)
    terms = jnp.where(lane == 0, high, jnp.where(lane == 1, mid, jnp.where(lane == 2, low, 0.0)))
    return jnp.pad(terms, ((0, 15), (0, width - value.shape[1]))).astype(BF16)


def local(real_feats, fake_feats, mix_num, w_first, bias, head):
    rows, d = real_feats.shape
    cols = w_first.shape[1]
    w_far = across(w_first)
    w = jnp.concatenate([w_first, w_far], axis=1)
    coef = mix_num.astype(F32) / 256.0
    real_f = real_feats.astype(F32)
    mixed = (real_f + coef[:, None] * (fake_feats.astype(F32) - real_f)).astype(BF16)
    vec = jnp.concatenate([bias, head])[None]
    far = across(vec)
    bias = jnp.concatenate([bias, far[0, :cols]])
    head = jnp.concatenate([head, far[0, cols:]])
    place = [lax.axis_index(k).astype(jnp.uint32) for k in ("x", "yl")]
    place = [((place[0] + k) & 3) * (d // 4) for k in range(4)] + [place[1], 1 - place[1]]
    group, _, place = gather_z(mixed, core(mixed), rows, place)
    z = tie(contract(group, w, ((1,), (0,)))) + bias
    sg = jax.nn.sigmoid(z)
    d1 = sg * (1.0 + z * (1.0 - sg))
    d2 = sg * (1.0 - sg) * (2.0 + z * (1.0 - 2.0 * sg))
    u = (d1 * head).astype(BF16)
    g = scatter_z(u, w, rows)
    norm = jnp.sqrt(jnp.sum(g * g, axis=1, keepdims=True) + 1e-06)
    scale = 20.0 * (norm - 1.0) / norm
    loss = jnp.sum(tie(jnp.broadcast_to((norm - 1.0) ** 2, (rows, 128))), axis=0, keepdims=True)
    mine = join((scale * g).astype(BF16), as_terms(loss, d))
    other = core(mine)
    tail = mine[rows:] + jnp.pad(other[rows:, :-3], ((0, 0), (3, 0)))
    big, tails, _ = gather_z(mine[:rows], join(other[:rows], tail), rows)
    p = tie(contract(big, w, ((1,), (0,))))
    dz = p * head * d2
    tails = [a[:1, :128].astype(F32) for a in tails]
    passed = tails[1] + tails[2] + tails[3]
    ends = tails[0] + tails[4]
    theirs = core(passed)
    loss = jnp.pad(ends + passed + theirs, ((0, 5), (0, cols - 128)))
    loss = jnp.concatenate([loss, loss], axis=1)
    sums = join(jnp.sum(dz, axis=0, keepdims=True), jnp.sum(p * d1, axis=0, keepdims=True), loss)
    grad_w, sums = scatter_w((group, big), (dz.astype(BF16), u), sums, place)
    penalty = 10.0 * jnp.sum(sums[2]) / (rows * 256)
    return (grad_w, sums[0], sums[1], penalty)


def solution(mesh):
    torus = Mesh(mesh.devices.reshape(4, 2, 8, 2, 2), ALL)
    hidden = ("z", "yh", "c")

    return jax.shard_map(
        local,
        mesh=torus,
        in_specs=(P(ALL, None), P(ALL, None), P(ALL), P(None, hidden), P(hidden), P(hidden)),
        out_specs=(P(("x", "yl"), hidden), P(hidden), P(hidden), P()),
        check_vma=False,
    )
```
